256 devices in a mesh: row: 16 (over z, y_hi), col: 16 (over x, y_lo, core).
Axes of the slice: x: 4, y: 4 (y_hi: 2, y_lo: 2; y = y_hi * 2 + y_lo), z: 8, core: 2. Of those that a mesh axis runs over, the one named last changes fastest.
Arguments:
- tokens: bfloat16 [1024, 14336], P('col', 'row'), may hold values from -6 to 6
- gate_weight: bfloat16 [14336, 26624], P('row', 'col'), may hold values from -0.046875 to 0.046875
- up_weight: bfloat16 [14336, 26624], P('row', 'col'), may hold values from -0.046875 to 0.046875
- upstream: bfloat16 [1024, 26624], P('row', 'col'), may hold values from -0.1875 to 0.1875
Outputs:
- grad_gate: bfloat16 [14336, 26624], P('row', 'col')
- grad_up: bfloat16 [14336, 26624], P('row', 'col')
The draws below stay inside these ranges and needn't reach their ends.
All inputs are finite; a program needn't handle non-finite values.
Results may differ from the reference program's by a relative error of at most 0.005.
Values may be sent and summed in bfloat16 or wider, within the bound.
A program may use at most 128 MiB of HBM per device.

```python
import jax
import jax.numpy as jnp
from jax import lax

D = 14336
FF = 26624
TOKENS = 1024


def levels(rng, extent, pieces, low, largest):
    def one(dim, blocks):
        draws = jax.random.uniform(jax.random.fold_in(jax.random.fold_in(rng, 6), dim), (blocks,), jnp.float32, low / len(pieces), largest / len(pieces))
        return jnp.repeat(jnp.exp(draws), extent[dim] // blocks).reshape((-1,) + (1,) * (len(extent) - dim - 1))

    gain = one(*pieces[0])
    for cut in pieces[1:]:
        gain = gain * one(*cut)
    return gain


def gaussian(own_key, extent, deviation, reach, shards=(), kind=jnp.bfloat16):
    values = deviation * jax.random.normal(own_key, extent, jnp.float32)
    if shards:
        values = values * levels(own_key, extent, shards, -0.22, 0.18)
    return jnp.clip(values, -reach, reach).astype(kind)


def setup_inputs(seed: int = 0) -> dict:
    keys = jax.random.split(jax.random.key(seed), 5)
    return {
        "tokens": gaussian(keys[0], (TOKENS, D), 1.0, 6.0, ((0, 16), (1, 16))),
        "gate_weight": gaussian(keys[1], (D, FF), D ** -0.5, 0.046875, ((0, 16), (1, 16))),
        "up_weight": gaussian(keys[2], (D, FF), D ** -0.5, 0.046875, ((0, 16), (1, 16))),
        "upstream": gaussian(keys[3], (TOKENS, FF), (TOKENS ** -0.5), 0.1875, ((0, 16), (1, 16))),
    }


def reference(tokens, gate_weight, up_weight, upstream):
    gate_pre = jnp.dot(tokens, gate_weight, preferred_element_type=jnp.float32)
    up_pre = jnp.dot(tokens, up_weight, preferred_element_type=jnp.float32)
    squash = jax.nn.sigmoid(gate_pre)
    cotangent = upstream.astype(jnp.float32)
    d_up = (cotangent * gate_pre * squash).astype(jnp.bfloat16)
    d_gate = (cotangent * up_pre * squash * (1.0 + gate_pre * (1.0 - squash))).astype(jnp.bfloat16)
    numbers = (((0,), (0,)), ((), ()))
    grad_gate = lax.dot_general(tokens, d_gate, numbers, preferred_element_type=jnp.float32).astype(jnp.bfloat16)
    grad_up = lax.dot_general(tokens, d_up, numbers, preferred_element_type=jnp.float32).astype(jnp.bfloat16)
    return (grad_gate, grad_up)
```

```python
import functools

import jax
import jax.numpy as jnp
from jax import lax
from jax.experimental import pallas as pl
from jax.experimental.pallas import tpu as pltpu
from jax.sharding import PartitionSpec as P

MESH = pl.DeviceIdType.MESH
F32 = jnp.float32
BF16 = jnp.bfloat16

NZ = 8
TB = 64
NT = 1024
DL = 896
FL = 1664
LANE = 128

ZT, YT = 6, 7
ZW, YW = ZT * LANE, YT * LANE
PHASES = ((3, 2), (2, 2), (2, 2))


def streams():
    out = []
    off, ycol, zcol = 0, 0, 0
    for ny, nz in PHASES:
        y = dict(kind="y", off=off, w=ny * LANE, col=ycol, gcol=ZW + ycol)
        off += 2 * ny * LANE
        ycol += ny * LANE
        zs = dict(kind="z", off=off, w=nz * LANE, col=zcol, gcol=zcol)
        off += 2 * nz * LANE
        zcol += nz * LANE
        out.append((y, zs))
    return out


def rcopy(src, dst, ssem, rsem, dev):
    return pltpu.make_async_remote_copy(
        src_ref=src, dst_ref=dst, send_sem=ssem, recv_sem=rsem, device_id=dev, device_id_type=MESH
    )


def kernel(
    x_ref, wg_ref, wu_ref, up_ref, gg_ref, gu_ref,
    xb, xt, wb, ub, zsz, zrz, zsy, zry, yown, ysend, yrecv, zfin, zfs, zfr, dall, gout,
    wsem, g_s, g_r, f_s, f_r, zz_s, zz_r, zy_s, zy_r, ye_s, ye_r, zf_s, zf_r,
    ay_s, ay_r, az_s, az_r, yf_s, yf_r, zx_s, zx_r, osem,
):
    row = lax.axis_index("row")
    col = lax.axis_index("col")
    z, h = lax.div(row, 2), lax.rem(row, 2)
    q, core = lax.div(col, 2), lax.rem(col, 2)
    zdev = ((lax.rem(z + 1, NZ) * 2 + h, col), (lax.rem(z + NZ - 1, NZ) * 2 + h, col))
    ydev = (z * 2 + 1 - h, col)
    cdev = (row, q * 2 + 1 - core)

    def qdev(i):
        return (row, lax.rem(q + i, NZ) * 2 + core)

    loads = [
        pltpu.make_async_copy(wg_ref.at[:, pl.ds(0, ZW)], wb.at[:, pl.ds(0, ZW)], wsem.at[0]),
        pltpu.make_async_copy(wu_ref.at[:, pl.ds(0, ZW)], wb.at[:, pl.ds(ZW, ZW)], wsem.at[1]),
        pltpu.make_async_copy(wg_ref.at[:, pl.ds(ZW, YW)], wb.at[:, pl.ds(2 * ZW, YW)], wsem.at[2]),
        pltpu.make_async_copy(wu_ref.at[:, pl.ds(ZW, YW)], wb.at[:, pl.ds(2 * ZW + YW, YW)], wsem.at[3]),
        pltpu.make_async_copy(up_ref, ub, wsem.at[4]),
    ]

    def xrows(c):
        return xb.at[pl.ds(pl.multiple_of(c * TB, TB), TB), :]

    own_x = pltpu.make_async_copy(x_ref, xrows(col), g_r.at[0])
    own_x.start()
    for c in loads:
        c.start()

    barrier = pltpu.get_barrier_semaphore()
    partners = [zdev[0], zdev[1], ydev, cdev] + [qdev(i) for i in range(1, NZ)]
    for dev in partners:
        pl.semaphore_signal(barrier, inc=1, device_id=dev, device_id_type=MESH)
    zrz[:, 0:2] = jnp.zeros((2, 2, 2 * TB, ZW), BF16)
    zry[:, 0:2] = jnp.zeros((2, 2, TB, YW), BF16)
    pl.semaphore_wait(barrier, len(partners))

    def gcopy(i):
        return rcopy(x_ref, xrows(col), g_s.at[i], g_r.at[i], qdev(i))

    for i in range(1, NZ):
        gcopy(i).start()

    def block_of(i):
        return lax.rem(q + NZ - i, NZ) * 2

    def fcopy(i):
        rows = xrows(block_of(i) + core)
        return rcopy(rows, rows, f_s.at[i], f_r.at[i], cdev)

    def fwait(i):
        rows = xrows(block_of(i) + 1 - core)
        return rcopy(rows, rows, f_s.at[i], f_r.at[i], cdev)

    for i in range(NZ):
        rows = xrows(block_of(i) + core)
        pltpu.make_async_copy(x_ref, rows, g_r.at[i]).wait()
        fcopy(i).start()
    for c in loads:
        c.wait()
    for i in range(NZ):
        fwait(i).wait_recv()

    def tokens_for(zz):
        a = pl.multiple_of(zz * 2 * TB + (1 - h) * TB, TB)
        b = pl.multiple_of(zz * 2 * TB + h * TB, TB)
        return jnp.concatenate([xb[pl.ds(a, TB), :], xb[pl.ds(b, TB), :]], axis=0)

    def zzcopy(d, t):
        return rcopy(zsz.at[d, t], zrz.at[d, t + 2], zz_s.at[d, t], zz_r.at[d, t], zdev[d])

    def zycopy(d, t):
        return rcopy(zsy.at[d, t], zry.at[d, t + 2], zy_s.at[d, t], zy_r.at[d, t], zdev[d])

    def yecopy(rel, half):
        return rcopy(ysend.at[rel, half], yrecv.at[rel, half], ye_s.at[rel, half], ye_r.at[rel, half], ydev)

    def zfcopy(half):
        return rcopy(zfs.at[half], zfr.at[half], zf_s.at[half], zf_r.at[half], ydev)

    def half_of(d, t):
        return lax.rem(t, 2) if d == 0 else 1 - lax.rem(t, 2)

    def rel_of(d, t):
        o = 4 - lax.rem(t, 2) - lax.div(t, 2)
        return o if d == 0 else NZ - o

    def z_step(t):
        for d in range(2):
            half = half_of(d, t)
            xd = tokens_for(lax.rem(z + rel_of(d, t), NZ))
            cols = pl.ds(pl.multiple_of(half * ZW, LANE), ZW)
            acc = jnp.dot(xd, wb[:, cols], preferred_element_type=F32)

            @pl.when(t >= 2)
            def _():
                zzcopy(d, t - 2).wait_recv()

            zsz[d, t] = (acc + zrz[d, t].astype(F32)).astype(BF16)
            zzcopy(d, t).start()

    def y_step(t):
        odd = lax.rem(t, 2)
        rel = (1 - odd) * (4 + lax.div(t, 2)) + odd * lax.div(7 - t, 2)
        zz = lax.rem(z + rel, NZ)
        xd = tokens_for(zz)
        for half in range(2):
            acc = jnp.dot(xd, wb[:, 2 * ZW + half * YW : 2 * ZW + (half + 1) * YW], preferred_element_type=F32)
            ysend[rel, half] = acc[:TB].astype(BF16)
            yecopy(rel, half).start()
            yown[rel, half] = acc[TB:]
        rows = pl.ds(pl.multiple_of(zz * 2 * TB, 2 * TB), 2 * TB)
        xt[:, rows] = xb[rows, :].T

    @pl.loop(0, NZ - 1)
    def _(t):
        z_step(t)
        y_step(t)

    y_step(jnp.int32(NZ - 1))

    def yz_step(t):
        for d in range(2):
            half = half_of(d, t)
            rel = rel_of(d, t)
            yecopy(rel, half).wait_recv()

            @pl.when(t >= 2)
            def _():
                zycopy(d, t - 2).wait_recv()

            acc = yown[rel, half] + yrecv[rel, half].astype(F32) + zry[d, t].astype(F32)
            zsy[d, t] = acc.astype(BF16)
            zycopy(d, t).start()

    @pl.loop(0, 3)
    def _(t):
        yz_step(t)

    for d in range(2):
        for t in (5, 6):
            zzcopy(d, t).wait_recv()
    xd = tokens_for(z)
    for half in range(2):
        acc = jnp.dot(xd, wb[:, half * ZW : (half + 1) * ZW], preferred_element_type=F32)
        acc = acc + zrz[0, 8 - half].astype(F32) + zrz[1, 7 + half].astype(F32)
        zfs[half] = acc[:TB].astype(BF16)
        zfcopy(half).start()
        zfin[half] = acc[TB:]

    @pl.loop(3, NZ - 1)
    def _(t):
        yz_step(t)

    my_rows = pl.ds(pl.multiple_of(row * TB, TB), TB)

    def store_grads(s, gate, up):
        w, off = s["w"], s["off"]
        u = ub[:, s["gcol"] : s["gcol"] + w].astype(F32)
        squash = jax.nn.sigmoid(gate)
        dall[my_rows, off : off + w] = (u * up * squash * (1.0 + gate * (1.0 - squash))).astype(BF16)
        dall[my_rows, off + w : off + 2 * w] = (u * gate * squash).astype(BF16)

    phases = streams()
    other_rows = pl.ds(pl.multiple_of((row + 1 - 2 * h) * TB, TB), TB)

    def zxcopy(p, rows):
        s = phases[p][1]
        ref = dall.at[rows, pl.ds(s["off"], 2 * s["w"])]
        return rcopy(ref, ref, zx_s.at[p], zx_r.at[p], ydev)

    def ag_slice(s, half, zz):
        cols = pl.ds(s["off"] + half * s["w"], s["w"])
        if s["kind"] == "y":
            return dall.at[pl.ds(pl.multiple_of(zz * 2 * TB + h * TB, TB), TB), cols]
        return dall.at[pl.ds(pl.multiple_of(zz * 2 * TB, 2 * TB), 2 * TB), cols]

    def agcopy(p, k, d, t, arriving=False):
        s = phases[p][k]
        half = t % 2 if d == 0 else 1 - t % 2
        hops = t // 2 + (1 if arriving else 0)
        zz = lax.rem(z + (NZ - hops if d == 0 else hops), NZ)
        ref = ag_slice(s, half, zz)
        ss, rs = ((ay_s, ay_r), (az_s, az_r))[k]
        return rcopy(ref, ref, ss.at[p, d, t], rs.at[p, d, t], zdev[d])

    def yfcopy(p, d, t, arriving=False):
        s = phases[p][0]
        if d == 2:
            half, zz, n = t, z, t
        else:
            half = t % 2 if d == 0 else 1 - t % 2
            hops = t // 2 + 1
            zz = lax.rem(z + (NZ - hops if d == 0 else hops), NZ)
            n = 2 + d * 7 + t
        hh = 1 - h if arriving else h
        ref = dall.at[
            pl.ds(pl.multiple_of(zz * 2 * TB + hh * TB, TB), TB), pl.ds(s["off"] + half * s["w"], s["w"])
        ]
        return rcopy(ref, ref, yf_s.at[p, n], yf_r.at[p, n], ydev)

    def out_copies(p, k):
        s = phases[p][k]
        off, w, g = s["off"], s["w"], s["gcol"]
        return [
            pltpu.make_async_copy(gout.at[:, pl.ds(off, w)], gg_ref.at[:, pl.ds(g, w)], osem.at[p, k, 0]),
            pltpu.make_async_copy(gout.at[:, pl.ds(off + w, w)], gu_ref.at[:, pl.ds(g, w)], osem.at[p, k, 1]),
        ]

    def weight_grads(p, k):
        s = phases[p][k]

        @pl.loop(0, 2 * s["w"] // 256)
        def _(n):
            cols = pl.ds(pl.multiple_of(s["off"] + n * 256, 256), 256)
            gout[:, cols] = jnp.dot(xt[...], dall[:, cols], preferred_element_type=F32).astype(BF16)

        for c in out_copies(p, k):
            c.start()

    def start_own(p, k):
        for t in range(2):
            for d in range(2):
                agcopy(p, k, d, t).start()
        if k == 0:
            for half in range(2):
                yfcopy(p, 2, half).start()

    def take(p, k, d, t):
        agcopy(p, k, d, t, arriving=True).wait_recv()
        if t < 5:
            agcopy(p, k, d, t + 2).start()
        if k == 0:
            yfcopy(p, d, t).start()

    def y_done(p):
        for half in range(2):
            yfcopy(p, 2, half, arriving=True).wait_recv()
        for t in range(7):
            for d in range(2):
                yfcopy(p, d, t, arriving=True).wait_recv()

    for half in range(2):
        zfcopy(half).wait_recv()
    for p, (_, s) in enumerate(phases):
        c = slice(s["col"], s["col"] + s["w"])
        store_grads(s, zfin[0, :, c] + zfr[0, :, c].astype(F32), zfin[1, :, c] + zfr[1, :, c].astype(F32))
        zxcopy(p, my_rows).start()

    for d in range(2):
        for t in (5, 6):
            zycopy(d, t).wait_recv()
    for half in range(2):
        yecopy(0, half).wait_recv()
    for p, (s, _) in enumerate(phases):
        c = slice(s["col"], s["col"] + s["w"])
        pre = [
            yown[0, a, :, c] + yrecv[0, a, :, c].astype(F32)
            + zry[0, 8 - a, :, c].astype(F32) + zry[1, 7 + a, :, c].astype(F32)
            for a in range(2)
        ]
        store_grads(s, pre[0], pre[1])
        if p == 0:
            start_own(0, 0)

    for p in range(len(phases)):
        if p == 0:
            zxcopy(0, other_rows).wait_recv()
            start_own(0, 1)
        for t in range(5):
            for k in range(2):
                for d in range(2):
                    take(p, k, d, t)
            if p and t == 1:
                weight_grads(p - 1, 1)
            if p and t == 3:
                y_done(p - 1)
                weight_grads(p - 1, 0)
        if p + 1 < len(phases):
            start_own(p + 1, 0)
            zxcopy(p + 1, other_rows).wait_recv()
            start_own(p + 1, 1)
        for t in (5, 6):
            for k in range(2):
                for d in range(2):
                    take(p, k, d, t)
    last = len(phases) - 1
    weight_grads(last, 1)
    y_done(last)
    weight_grads(last, 0)

    for i in range(1, NZ):
        gcopy(i).wait_send()
    for i in range(NZ):
        fcopy(i).wait_send()

    @pl.loop(0, 7)
    def _(t):
        for d in range(2):
            zzcopy(d, t).wait_send()
            zycopy(d, t).wait_send()

    @pl.loop(0, NZ)
    def _(rel):
        for half in range(2):
            yecopy(rel, half).wait_send()

    for half in range(2):
        zfcopy(half).wait_send()
    for p in range(len(phases)):
        zxcopy(p, my_rows).wait_send()
        for t in range(7):
            for d in range(2):
                for k in range(2):
                    agcopy(p, k, d, t).wait_send()
                yfcopy(p, d, t).wait_send()
        for half in range(2):
            yfcopy(p, 2, half).wait_send()
        for k in range(2):
            for c in out_copies(p, k):
                c.wait()


def local(tokens, gate_weight, up_weight, upstream):
    n = len(PHASES)
    dma = pltpu.SemaphoreType.DMA
    any_spec = pl.BlockSpec(memory_space=pl.ANY)
    return pl.pallas_call(
        kernel,
        out_shape=(jax.ShapeDtypeStruct((DL, FL), BF16), jax.ShapeDtypeStruct((DL, FL), BF16)),
        in_specs=[any_spec] * 4,
        out_specs=(any_spec, any_spec),
        scratch_shapes=[
            pltpu.VMEM((NT, DL), BF16),
            pltpu.VMEM((DL, NT), BF16),
            pltpu.VMEM((DL, 2 * FL), BF16),
            pltpu.VMEM((TB, FL), BF16),
            pltpu.VMEM((2, 7, 2 * TB, ZW), BF16),
            pltpu.VMEM((2, 9, 2 * TB, ZW), BF16),
            pltpu.VMEM((2, 7, TB, YW), BF16),
            pltpu.VMEM((2, 9, TB, YW), BF16),
            pltpu.VMEM((NZ, 2, TB, YW), F32),
            pltpu.VMEM((NZ, 2, TB, YW), BF16),
            pltpu.VMEM((NZ, 2, TB, YW), BF16),
            pltpu.VMEM((2, TB, ZW), F32),
            pltpu.VMEM((2, TB, ZW), BF16),
            pltpu.VMEM((2, TB, ZW), BF16),
            pltpu.VMEM((NT, 2 * FL), BF16),
            pltpu.VMEM((DL, 2 * FL), BF16),
            dma((5,)),
            dma((NZ,)), dma((NZ,)),
            dma((NZ,)), dma((NZ,)),
            dma((2, 7)), dma((2, 7)),
            dma((2, 7)), dma((2, 7)),
            dma((NZ, 2)), dma((NZ, 2)),
            dma((2,)), dma((2,)),
            dma((n, 2, 7)), dma((n, 2, 7)),
            dma((n, 2, 7)), dma((n, 2, 7)),
            dma((n, 16)), dma((n, 16)),
            dma((n,)), dma((n,)),
            dma((n, 2, 2)),
        ],
        compiler_params=pltpu.CompilerParams(
            collective_id=0, has_side_effects=True, vmem_limit_bytes=60 * 1024 * 1024
        ),
    )(tokens, gate_weight, up_weight, upstream)


def solution(mesh):
    return jax.shard_map(
        local,
        mesh=mesh,
        in_specs=(P("col", "row"), P("row", "col"), P("row", "col"), P("row", "col")),
        out_specs=(P("row", "col"), P("row", "col")),
        check_vma=False,
    )
```

```python
import functools

import jax
import jax.numpy as jnp
from jax import lax
from jax.experimental import pallas as pl
from jax.experimental.pallas import tpu as pltpu
from jax.sharding import PartitionSpec as P

MESH = pl.DeviceIdType.MESH
F32 = jnp.float32
BF16 = jnp.bfloat16

NZ = 8
TB = 64
NT = 1024
DL = 896
FL = 1664
LANE = 128

ZT, YT = 6, 7
ZW, YW = ZT * LANE, YT * LANE
PHASES = ((3, 2), (2, 2), (2, 2))


def streams():
    out = []
    off, ycol, zcol = 0, 0, 0
    for ny, nz in PHASES:
        y = dict(kind="y", off=off, w=ny * LANE, col=ycol, gcol=ZW + ycol)
        off += 2 * ny * LANE
        ycol += ny * LANE
        zs = dict(kind="z", off=off, w=nz * LANE, col=zcol, gcol=zcol)
        off += 2 * nz * LANE
        zcol += nz * LANE
        out.append((y, zs))
    return out


def rcopy(src, dst, ssem, rsem, dev):
    return pltpu.make_async_remote_copy(
        src_ref=src, dst_ref=dst, send_sem=ssem, recv_sem=rsem, device_id=dev, device_id_type=MESH
    )


def kernel(
    x_ref, wg_ref, wu_ref, up_ref, gout, xt, dall,
    xb, wb, ub, zsz, zrz, zsy, zry, yown, ysend, yrecv, zfin, zfs, zfr,
    wsem, g_s, g_r, f_s, f_r, zz_s, zz_r, zy_s, zy_r, ye_s, ye_r, zf_s, zf_r,
    ay_s, ay_r, az_s, az_r, yf_s, yf_r, zx_s, zx_r,
):
    row = lax.axis_index("row")
    col = lax.axis_index("col")
    z, h = lax.div(row, 2), lax.rem(row, 2)
    q, core = lax.div(col, 2), lax.rem(col, 2)
    zdev = ((lax.rem(z + 1, NZ) * 2 + h, col), (lax.rem(z + NZ - 1, NZ) * 2 + h, col))
    ydev = (z * 2 + 1 - h, col)
    cdev = (row, q * 2 + 1 - core)

    xx, yl = lax.div(q, 2), lax.rem(q, 2)
    ql = q + 1 - 2 * yl
    ldev = (row, ql * 2 + core)

    def xdev(i):
        return (row, (lax.rem(xx + i, 4) * 2 + yl) * 2 + core)

    loads = [
        pltpu.make_async_copy(wg_ref.at[:, pl.ds(ZW, YW)], wb.at[:, pl.ds(2 * ZW, YW)], wsem.at[2]),
        pltpu.make_async_copy(wu_ref.at[:, pl.ds(ZW, YW)], wb.at[:, pl.ds(2 * ZW + YW, YW)], wsem.at[3]),
        pltpu.make_async_copy(wg_ref.at[:, pl.ds(0, ZW)], wb.at[:, pl.ds(0, ZW)], wsem.at[0]),
        pltpu.make_async_copy(wu_ref.at[:, pl.ds(0, ZW)], wb.at[:, pl.ds(ZW, ZW)], wsem.at[1]),
        pltpu.make_async_copy(up_ref, ub, wsem.at[4]),
    ]

    def xrows(c):
        return xb.at[pl.ds(pl.multiple_of(c * TB, TB), TB), :]

    own_x = pltpu.make_async_copy(x_ref, xrows(col), g_r.at[q])
    own_x.start()
    for c in loads:
        c.start()

    barrier = pltpu.get_barrier_semaphore()
    partners = [zdev[0], zdev[1], ydev, cdev, ldev, xdev(1), xdev(2), xdev(3)]
    for dev in partners:
        pl.semaphore_signal(barrier, inc=1, device_id=dev, device_id_type=MESH)
    zrz[:, 0:2] = jnp.zeros((2, 2, 2 * TB, ZW), BF16)
    zry[:, 0:2] = jnp.zeros((2, 2, TB, YW), BF16)
    pl.semaphore_wait(barrier, len(partners))

    def own_copy(n, dev):
        return rcopy(x_ref, xrows(col), g_s.at[n], g_r.at[q], dev)

    def pass_copy(n, dev):
        rows = xrows(ql * 2 + core)
        return rcopy(rows, rows, g_s.at[n], g_r.at[ql], dev)

    def fcopy(b):
        rows = xrows(b * 2 + core)
        return rcopy(rows, rows, f_s.at[b], f_r.at[b], cdev)

    own_core = rcopy(x_ref, xrows(col), f_s.at[q], f_r.at[q], cdev)

    def fwait(b):
        rows = xrows(b * 2 + 1 - core)
        rcopy(rows, rows, f_s.at[b], f_r.at[b], cdev).wait_recv()

    def gwait(b):
        pltpu.make_async_copy(x_ref, xrows(b * 2 + core), g_r.at[b]).wait()

    def send_own():
        for i in (2, 1, 3):
            own_copy(i, xdev(i)).start()

    def send_neighbour():
        gwait(ql)
        for i in (2, 1, 3):
            pass_copy(3 + i, xdev(i)).start()
        fcopy(ql).start()

    own_copy(0, ldev).start()
    own_core.start()
    first = lax.rem(z + 4, NZ)

    @pl.when(ql == first)
    def _():
        send_neighbour()

    send_own()
    gwait(q)
    for c in loads:
        c.wait()
    fwait(q)

    def arrive(b):
        @pl.when(jnp.logical_and(b != q, b != ql))
        def _():
            gwait(b)
            fcopy(b).start()

    def arrived(b):
        @pl.when(b != q)
        def _():
            fwait(b)

    def tokens_for(zz):
        a = pl.multiple_of(zz * 2 * TB + (1 - h) * TB, TB)
        b = pl.multiple_of(zz * 2 * TB + h * TB, TB)
        return jnp.concatenate([xb[pl.ds(a, TB), :], xb[pl.ds(b, TB), :]], axis=0)

    def zzcopy(d, t):
        return rcopy(zsz.at[d, t], zrz.at[d, t + 2], zz_s.at[d, t], zz_r.at[d, t], zdev[d])

    def zycopy(d, t):
        return rcopy(zsy.at[d, t], zry.at[d, t + 2], zy_s.at[d, t], zy_r.at[d, t], zdev[d])

    def yecopy(rel, half):
        return rcopy(ysend.at[rel, half], yrecv.at[rel, half], ye_s.at[rel, half], ye_r.at[rel, half], ydev)

    def zfcopy(half):
        return rcopy(zfs.at[half], zfr.at[half], zf_s.at[half], zf_r.at[half], ydev)

    def half_of(d, t):
        return lax.rem(t, 2) if d == 0 else 1 - lax.rem(t, 2)

    def rel_of(d, t):
        o = 4 - lax.rem(t, 2) - lax.div(t, 2)
        return o if d == 0 else NZ - o

    def z_step(t):
        for d in range(2):
            half = half_of(d, t)
            xd = tokens_for(lax.rem(z + rel_of(d, t), NZ))
            cols = pl.ds(pl.multiple_of(half * ZW, LANE), ZW)
            acc = jnp.dot(xd, wb[:, cols], preferred_element_type=F32)

            @pl.when(t >= 2)
            def _():
                zzcopy(d, t - 2).wait_recv()

            zsz[d, t] = (acc + zrz[d, t].astype(F32)).astype(BF16)
            zzcopy(d, t).start()

    def y_part(rel):
        zz = lax.rem(z + rel, NZ)
        xd = tokens_for(zz)
        for half in range(2):
            acc = jnp.dot(xd, wb[:, 2 * ZW + half * YW : 2 * ZW + (half + 1) * YW], preferred_element_type=F32)
            ysend[rel, half] = acc[:TB].astype(BF16)
            yecopy(rel, half).start()
            yown[rel, half] = acc[TB:]
        rows = pl.ds(pl.multiple_of(zz * 2 * TB, 2 * TB), 2 * TB)
        xt[:, rows] = xb[rows, :].T

    def rel_at(j):
        odd = lax.rem(j, 2)
        return (1 - odd) * (4 + lax.div(j, 2)) + odd * lax.div(7 - j, 2)

    def y_step(j):
        rel = rel_at(j)

        @pl.when(rel != rel_q)
        def _():
            y_part(rel)

    def block(j):
        return lax.rem(z + rel_at(jnp.int32(j)), NZ)

    rel_q = lax.rem(q + NZ - z, NZ)
    y_part(rel_q)

    @pl.when(ql != first)
    def _():
        send_neighbour()

    arrive(block(0))
    arrived(block(0))
    z_step(jnp.int32(0))
    for j in range(1, NZ):
        arrive(block(j))
    y_step(jnp.int32(0))
    for j in range(1, NZ):
        arrived(block(j))

    @pl.loop(1, NZ - 1)
    def _(t):
        z_step(t)
        y_step(t)

    y_step(jnp.int32(NZ - 1))

    def yz_step(t):
        for d in range(2):
            half = half_of(d, t)
            rel = rel_of(d, t)
            yecopy(rel, half).wait_recv()

            @pl.when(t >= 2)
            def _():
                zycopy(d, t - 2).wait_recv()

            acc = yown[rel, half] + yrecv[rel, half].astype(F32) + zry[d, t].astype(F32)
            zsy[d, t] = acc.astype(BF16)
            zycopy(d, t).start()

    @pl.loop(0, 3)
    def _(t):
        yz_step(t)

    for d in range(2):
        for t in (5, 6):
            zzcopy(d, t).wait_recv()
    xd = tokens_for(z)
    for half in range(2):
        acc = jnp.dot(xd, wb[:, half * ZW : (half + 1) * ZW], preferred_element_type=F32)
        acc = acc + zrz[0, 8 - half].astype(F32) + zrz[1, 7 + half].astype(F32)
        zfs[half] = acc[:TB].astype(BF16)
        zfcopy(half).start()
        zfin[half] = acc[TB:]

    @pl.loop(3, NZ - 1)
    def _(t):
        yz_step(t)

    my_rows = pl.ds(pl.multiple_of(row * TB, TB), TB)

    def store_grads(s, gate, up):
        w, off = s["w"], s["off"]
        u = ub[:, s["gcol"] : s["gcol"] + w].astype(F32)
        squash = jax.nn.sigmoid(gate)
        dall[my_rows, off : off + w] = (u * up * squash * (1.0 + gate * (1.0 - squash))).astype(BF16)
        dall[my_rows, off + w : off + 2 * w] = (u * gate * squash).astype(BF16)

    phases = streams()
    other_rows = pl.ds(pl.multiple_of((row + 1 - 2 * h) * TB, TB), TB)

    def zxcopy(p, rows):
        s = phases[p][1]
        ref = dall.at[rows, pl.ds(s["off"], 2 * s["w"])]
        return rcopy(ref, ref, zx_s.at[p], zx_r.at[p], ydev)

    def ag_slice(s, half, zz):
        cols = pl.ds(s["off"] + half * s["w"], s["w"])
        if s["kind"] == "y":
            return dall.at[pl.ds(pl.multiple_of(zz * 2 * TB + h * TB, TB), TB), cols]
        return dall.at[pl.ds(pl.multiple_of(zz * 2 * TB, 2 * TB), 2 * TB), cols]

    def agcopy(p, k, d, t, arriving=False):
        s = phases[p][k]
        half = t % 2 if d == 0 else 1 - t % 2
        hops = t // 2 + (1 if arriving else 0)
        zz = lax.rem(z + (NZ - hops if d == 0 else hops), NZ)
        ref = ag_slice(s, half, zz)
        ss, rs = ((ay_s, ay_r), (az_s, az_r))[k]
        return rcopy(ref, ref, ss.at[p, d, t], rs.at[p, d, t], zdev[d])

    def yfcopy(p, d, t, arriving=False):
        s = phases[p][0]
        if d == 2:
            half, zz, n = t, z, t
        else:
            half = t % 2 if d == 0 else 1 - t % 2
            hops = t // 2 + 1
            zz = lax.rem(z + (NZ - hops if d == 0 else hops), NZ)
            n = 2 + d * 7 + t
        hh = 1 - h if arriving else h
        ref = dall.at[
            pl.ds(pl.multiple_of(zz * 2 * TB + hh * TB, TB), TB), pl.ds(s["off"] + half * s["w"], s["w"])
        ]
        return rcopy(ref, ref, yf_s.at[p, n], yf_r.at[p, n], ydev)

    def weight_grads(p, k):
        s = phases[p][k]

        @pl.loop(0, 2 * s["w"] // 256)
        def _(n):
            cols = pl.ds(pl.multiple_of(s["off"] + n * 256, 256), 256)
            gout[:, cols] = jnp.dot(xt[...], dall[:, cols], preferred_element_type=F32).astype(BF16)


    def start_own(p, k):
        for t in range(2):
            for d in range(2):
                agcopy(p, k, d, t).start()
        if k == 0:
            for half in range(2):
                yfcopy(p, 2, half).start()

    def take(p, k, d, t):
        agcopy(p, k, d, t, arriving=True).wait_recv()
        if t < 5:
            agcopy(p, k, d, t + 2).start()
        if k == 0:
            yfcopy(p, d, t).start()

    def y_done(p):
        for half in range(2):
            yfcopy(p, 2, half, arriving=True).wait_recv()
        for t in range(7):
            for d in range(2):
                yfcopy(p, d, t, arriving=True).wait_recv()

    for half in range(2):
        zfcopy(half).wait_recv()
    for p, (_, s) in enumerate(phases):
        c = slice(s["col"], s["col"] + s["w"])
        store_grads(s, zfin[0, :, c] + zfr[0, :, c].astype(F32), zfin[1, :, c] + zfr[1, :, c].astype(F32))
        zxcopy(p, my_rows).start()

    for d in range(2):
        for t in (5, 6):
            zycopy(d, t).wait_recv()
    for half in range(2):
        yecopy(0, half).wait_recv()
    for p, (s, _) in enumerate(phases):
        c = slice(s["col"], s["col"] + s["w"])
        pre = [
            yown[0, a, :, c] + yrecv[0, a, :, c].astype(F32)
            + zry[0, 8 - a, :, c].astype(F32) + zry[1, 7 + a, :, c].astype(F32)
            for a in range(2)
        ]
        store_grads(s, pre[0], pre[1])
        if p == 0:
            start_own(0, 0)

    for p in range(len(phases)):
        if p == 0:
            zxcopy(0, other_rows).wait_recv()
            start_own(0, 1)
        for t in range(5):
            for k in range(2):
                for d in range(2):
                    take(p, k, d, t)
            if p and t == 1:
                weight_grads(p - 1, 1)
            if p and t == 3:
                y_done(p - 1)
                weight_grads(p - 1, 0)
        if p + 1 < len(phases):
            start_own(p + 1, 0)
            zxcopy(p + 1, other_rows).wait_recv()
            start_own(p + 1, 1)
        for t in (5, 6):
            for k in range(2):
                for d in range(2):
                    take(p, k, d, t)
    last = len(phases) - 1
    y_done(last)

    own_copy(0, ldev).wait_send()
    for i in (2, 1, 3):
        own_copy(i, xdev(i)).wait_send()
        pass_copy(3 + i, xdev(i)).wait_send()
    for i in range(NZ):
        fcopy(jnp.int32(i)).wait_send()

    @pl.loop(0, 7)
    def _(t):
        for d in range(2):
            zzcopy(d, t).wait_send()
            zycopy(d, t).wait_send()

    @pl.loop(0, NZ)
    def _(rel):
        for half in range(2):
            yecopy(rel, half).wait_send()

    for half in range(2):
        zfcopy(half).wait_send()
    for p in range(len(phases)):
        zxcopy(p, my_rows).wait_send()
        for t in range(7):
            for d in range(2):
                for k in range(2):
                    agcopy(p, k, d, t).wait_send()
                yfcopy(p, d, t).wait_send()
        for half in range(2):
            yfcopy(p, 2, half).wait_send()


def finish(gout, xt, dall, gg_ref, gu_ref, late, osem):
    phases = streams()
    last = len(phases) - 1
    base = phases[last][0]["off"]
    copies = []

    def send(p, k, src, off):
        s = phases[p][k]
        w, g = s["w"], s["gcol"]
        for a, ref in enumerate((gg_ref, gu_ref)):
            c = pltpu.make_async_copy(src.at[:, pl.ds(off + a * w, w)], ref.at[:, pl.ds(g, w)], osem.at[p, k, a])
            c.start()
            copies.append(c)

    for p in range(last):
        for k in range(2):
            send(p, k, gout, phases[p][k]["off"])
    for k in range(2):
        s = phases[last][k]

        @pl.loop(0, 2 * s["w"] // 256)
        def _(n):
            src = pl.ds(pl.multiple_of(s["off"] + n * 256, 256), 256)
            dst = pl.ds(pl.multiple_of(s["off"] - base + n * 256, 256), 256)
            late[:, dst] = jnp.dot(xt[...], dall[:, src], preferred_element_type=F32).astype(BF16)

        send(last, k, late, s["off"] - base)
    for c in copies:
        c.wait()


def local(tokens, gate_weight, up_weight, upstream):
    n = len(PHASES)
    dma = pltpu.SemaphoreType.DMA
    any_spec = pl.BlockSpec(memory_space=pl.ANY)
    vmem_spec = pl.BlockSpec(memory_space=pltpu.VMEM)
    gout, xt, dall = pl.pallas_call(
        kernel,
        out_shape=(pltpu.VMEM((DL, 2 * FL), BF16), pltpu.VMEM((DL, NT), BF16), pltpu.VMEM((NT, 2 * FL), BF16)),
        in_specs=[any_spec] * 4,
        out_specs=(vmem_spec,) * 3,
        scratch_shapes=[
            pltpu.VMEM((NT, DL), BF16),
            pltpu.VMEM((DL, 2 * FL), BF16),
            pltpu.VMEM((TB, FL), BF16),
            pltpu.VMEM((2, 7, 2 * TB, ZW), BF16),
            pltpu.VMEM((2, 9, 2 * TB, ZW), BF16),
            pltpu.VMEM((2, 7, TB, YW), BF16),
            pltpu.VMEM((2, 9, TB, YW), BF16),
            pltpu.VMEM((NZ, 2, TB, YW), F32),
            pltpu.VMEM((NZ, 2, TB, YW), BF16),
            pltpu.VMEM((NZ, 2, TB, YW), BF16),
            pltpu.VMEM((2, TB, ZW), F32),
            pltpu.VMEM((2, TB, ZW), BF16),
            pltpu.VMEM((2, TB, ZW), BF16),
            dma((5,)),
            dma((NZ,)), dma((NZ,)),
            dma((NZ,)), dma((NZ,)),
            dma((2, 7)), dma((2, 7)),
            dma((2, 7)), dma((2, 7)),
            dma((NZ, 2)), dma((NZ, 2)),
            dma((2,)), dma((2,)),
            dma((n, 2, 7)), dma((n, 2, 7)),
            dma((n, 2, 7)), dma((n, 2, 7)),
            dma((n, 16)), dma((n, 16)),
            dma((n,)), dma((n,)),
        ],
        compiler_params=pltpu.CompilerParams(
            collective_id=0, has_side_effects=True, vmem_limit_bytes=44 * 1024 * 1024
        ),
    )(tokens, gate_weight, up_weight, upstream)
    width = sum(2 * s["w"] for s in streams()[-1])
    return pl.pallas_call(
        finish,
        out_shape=(jax.ShapeDtypeStruct((DL, FL), BF16), jax.ShapeDtypeStruct((DL, FL), BF16)),
        in_specs=[vmem_spec] * 3,
        out_specs=(any_spec, any_spec),
        scratch_shapes=[pltpu.VMEM((DL, width), BF16), dma((n, 2, 2))],
        compiler_params=pltpu.CompilerParams(vmem_limit_bytes=4 * 1024 * 1024),
    )(gout, xt, dall)


def solution(mesh):
    return jax.shard_map(
        local,
        mesh=mesh,
        in_specs=(P("col", "row"), P("row", "col"), P("row", "col"), P("row", "col")),
        out_specs=(P("row", "col"), P("row", "col")),
        check_vma=False,
    )
```

```python
import functools

import jax
import jax.numpy as jnp
from jax import lax
from jax.experimental import pallas as pl
from jax.experimental.pallas import tpu as pltpu
from jax.sharding import PartitionSpec as P

MESH = pl.DeviceIdType.MESH
F32 = jnp.float32
BF16 = jnp.bfloat16

NZ = 8
TB = 64
NT = 1024
DL = 896
FL = 1664
LANE = 128

ZT, YT = 5, 8
ZW, YW = ZT * LANE, YT * LANE
PHASES = ((5, 3), (2, 3))


def streams():
    out = []
    off, zt, yt = 0, 0, sum(nz for _, nz in PHASES)
    for ny, nz in PHASES:
        y = dict(kind="y", off=off, w=ny * LANE, gcol=yt * LANE)
        off += 2 * ny * LANE
        yt += ny
        zs = dict(kind="z", off=off, w=nz * LANE, gcol=zt * LANE)
        off += 2 * nz * LANE
        zt += nz
        out.append((y, zs))
    return out


def rcopy(src, dst, ssem, rsem, dev):
    return pltpu.make_async_remote_copy(
        src_ref=src, dst_ref=dst, send_sem=ssem, recv_sem=rsem, device_id=dev, device_id_type=MESH
    )


def kernel(
    x_ref, wg_ref, wu_ref, up_ref, gout, xt, dall,
    xb, wb, ub, zsz, zrz, zsy, zry, yown, ysend, yrecv, zfin, zfs, zfr,
    wsem, g_s, g_r, f_s, f_r, zz_s, zz_r, zy_s, zy_r, ye_s, ye_r, zf_s, zf_r,
    ay_s, ay_r, az_s, az_r, yf_s, yf_r, zx_s, zx_r,
):
    row = lax.axis_index("row")
    col = lax.axis_index("col")
    z, h = lax.div(row, 2), lax.rem(row, 2)
    q, core = lax.div(col, 2), lax.rem(col, 2)
    zdev = ((lax.rem(z + 1, NZ) * 2 + h, col), (lax.rem(z + NZ - 1, NZ) * 2 + h, col))
    ydev = (z * 2 + 1 - h, col)
    cdev = (row, q * 2 + 1 - core)

    xx, yl = lax.div(q, 2), lax.rem(q, 2)
    ql = q + 1 - 2 * yl
    ldev = (row, ql * 2 + core)

    def xdev(i):
        return (row, (lax.rem(xx + i, 4) * 2 + yl) * 2 + core)

    loads = [
        pltpu.make_async_copy(wg_ref.at[:, pl.ds(ZW, YW)], wb.at[:, pl.ds(2 * ZW, YW)], wsem.at[2]),
        pltpu.make_async_copy(wu_ref.at[:, pl.ds(ZW, YW)], wb.at[:, pl.ds(2 * ZW + YW, YW)], wsem.at[3]),
        pltpu.make_async_copy(wg_ref.at[:, pl.ds(0, ZW)], wb.at[:, pl.ds(0, ZW)], wsem.at[0]),
        pltpu.make_async_copy(wu_ref.at[:, pl.ds(0, ZW)], wb.at[:, pl.ds(ZW, ZW)], wsem.at[1]),
        pltpu.make_async_copy(up_ref, ub, wsem.at[4]),
    ]

    def xrows(c):
        return xb.at[pl.ds(pl.multiple_of(c * TB, TB), TB), :]

    own_x = pltpu.make_async_copy(x_ref, xrows(col), g_r.at[q])
    own_x.start()
    for c in loads:
        c.start()

    barrier = pltpu.get_barrier_semaphore()
    partners = [zdev[0], zdev[1], ydev, cdev, ldev, xdev(1), xdev(2), xdev(3)]
    for dev in partners:
        pl.semaphore_signal(barrier, inc=1, device_id=dev, device_id_type=MESH)
    zrz[:, 0:2] = jnp.zeros((2, 2, 2 * TB, ZW), BF16)
    zry[:, 0:2] = jnp.zeros((2, 2, TB, YW), BF16)
    pl.semaphore_wait(barrier, len(partners))

    def own_copy(n, dev):
        return rcopy(x_ref, xrows(col), g_s.at[n], g_r.at[q], dev)

    def pass_copy(n, dev):
        rows = xrows(ql * 2 + core)
        return rcopy(rows, rows, g_s.at[n], g_r.at[ql], dev)

    def fcopy(b):
        rows = xrows(b * 2 + core)
        return rcopy(rows, rows, f_s.at[b], f_r.at[b], cdev)

    own_core = rcopy(x_ref, xrows(col), f_s.at[q], f_r.at[q], cdev)

    def fwait(b):
        rows = xrows(b * 2 + 1 - core)
        rcopy(rows, rows, f_s.at[b], f_r.at[b], cdev).wait_recv()

    def gwait(b):
        pltpu.make_async_copy(x_ref, xrows(b * 2 + core), g_r.at[b]).wait()

    def send_own():
        for i in (2, 1, 3):
            own_copy(i, xdev(i)).start()

    def send_neighbour():
        gwait(ql)
        for i in (2, 1, 3):
            pass_copy(3 + i, xdev(i)).start()
        fcopy(ql).start()

    own_copy(0, ldev).start()
    own_core.start()
    first = lax.rem(z + 4, NZ)

    @pl.when(ql == first)
    def _():
        send_neighbour()

    send_own()
    gwait(q)
    for c in loads:
        c.wait()
    fwait(q)

    def arrive(b):
        @pl.when(jnp.logical_and(b != q, b != ql))
        def _():
            gwait(b)
            fcopy(b).start()

    def arrived(b):
        @pl.when(b != q)
        def _():
            fwait(b)

    def tokens_for(zz):
        a = pl.multiple_of(zz * 2 * TB + (1 - h) * TB, TB)
        b = pl.multiple_of(zz * 2 * TB + h * TB, TB)
        return jnp.concatenate([xb[pl.ds(a, TB), :], xb[pl.ds(b, TB), :]], axis=0)

    def zzcopy(d, t):
        return rcopy(zsz.at[d, t], zrz.at[d, t + 2], zz_s.at[d, t], zz_r.at[d, t], zdev[d])

    def zycopy(d, t):
        return rcopy(zsy.at[d, t], zry.at[d, t + 2], zy_s.at[d, t], zy_r.at[d, t], zdev[d])

    def yecopy(rel, half):
        return rcopy(ysend.at[rel, half], yrecv.at[rel, half], ye_s.at[rel, half], ye_r.at[rel, half], ydev)

    def zfcopy(half):
        return rcopy(zfs.at[half], zfr.at[half], zf_s.at[half], zf_r.at[half], ydev)

    def half_of(d, t):
        return lax.rem(t, 2) if d == 0 else 1 - lax.rem(t, 2)

    def rel_of(d, t):
        o = 4 - lax.rem(t, 2) - lax.div(t, 2)
        return o if d == 0 else NZ - o

    def z_step(t):
        for d in range(2):
            half = half_of(d, t)
            xd = tokens_for(lax.rem(z + rel_of(d, t), NZ))
            cols = pl.ds(pl.multiple_of(half * ZW, LANE), ZW)
            acc = jnp.dot(xd, wb[:, cols], preferred_element_type=F32)

            @pl.when(t >= 2)
            def _():
                zzcopy(d, t - 2).wait_recv()

            zsz[d, t] = (acc + zrz[d, t].astype(F32)).astype(BF16)
            zzcopy(d, t).start()

    def y_part(rel):
        zz = lax.rem(z + rel, NZ)
        xd = tokens_for(zz)
        for half in range(2):
            acc = jnp.dot(xd, wb[:, 2 * ZW + half * YW : 2 * ZW + (half + 1) * YW], preferred_element_type=F32)
            ysend[rel, half] = acc[:TB].astype(BF16)
            yecopy(rel, half).start()
            yown[rel, half] = acc[TB:]
        rows = pl.ds(pl.multiple_of(zz * 2 * TB, 2 * TB), 2 * TB)
        xt[:, rows] = xb[rows, :].T

    def rel_at(j):
        odd = lax.rem(j, 2)
        return (1 - odd) * (4 + lax.div(j, 2)) + odd * lax.div(7 - j, 2)

    def y_step(j):
        rel = rel_at(j)

        @pl.when(rel != rel_q)
        def _():
            y_part(rel)

    def block(j):
        return lax.rem(z + rel_at(jnp.int32(j)), NZ)

    rel_q = lax.rem(q + NZ - z, NZ)
    y_part(rel_q)

    @pl.when(ql != first)
    def _():
        send_neighbour()

    arrive(block(0))
    arrived(block(0))
    z_step(jnp.int32(0))
    for j in range(1, NZ):
        arrive(block(j))
    y_step(jnp.int32(0))
    for j in range(1, NZ):
        arrived(block(j))

    @pl.loop(1, NZ - 1)
    def _(t):
        z_step(t)
        y_step(t)

    y_step(jnp.int32(NZ - 1))

    def yz_step(t):
        for d in range(2):
            half = half_of(d, t)
            rel = rel_of(d, t)
            yecopy(rel, half).wait_recv()

            @pl.when(t >= 2)
            def _():
                zycopy(d, t - 2).wait_recv()

            acc = yown[rel, half] + yrecv[rel, half].astype(F32) + zry[d, t].astype(F32)
            zsy[d, t] = acc.astype(BF16)
            zycopy(d, t).start()

    @pl.loop(0, 3)
    def _(t):
        yz_step(t)

    for d in range(2):
        for t in (5, 6):
            zzcopy(d, t).wait_recv()
    xd = tokens_for(z)
    for half in range(2):
        acc = jnp.dot(xd, wb[:, half * ZW : (half + 1) * ZW], preferred_element_type=F32)
        acc = acc + zrz[0, 8 - half].astype(F32) + zrz[1, 7 + half].astype(F32)
        zfs[half] = acc[:TB].astype(BF16)
        zfcopy(half).start()
        zfin[half] = acc[TB:]

    @pl.loop(3, NZ - 1)
    def _(t):
        yz_step(t)

    my_rows = pl.ds(pl.multiple_of(row * TB, TB), TB)
    phases = streams()

    def store_grads(lo, hi, pre):
        for s in (s for phase in phases for s in phase):
            a, b = max(lo, s["gcol"]), min(hi, s["gcol"] + s["w"])
            if a >= b:
                continue
            gate, up = pre(0, a - lo, b - lo), pre(1, a - lo, b - lo)
            off = s["off"] + a - s["gcol"]
            u = ub[:, a:b].astype(F32)
            squash = jax.nn.sigmoid(gate)
            dall[my_rows, off : off + b - a] = (
                u * up * squash * (1.0 + gate * (1.0 - squash))
            ).astype(BF16)
            off += s["w"]
            dall[my_rows, off : off + b - a] = (u * gate * squash).astype(BF16)

    def z_pre(half, a, b):
        return zfin[half, :, a:b] + zfr[half, :, a:b].astype(F32)

    def y_pre(half, a, b):
        return (
            yown[0, half, :, a:b] + yrecv[0, half, :, a:b].astype(F32)
            + zry[0, 8 - half, :, a:b].astype(F32) + zry[1, 7 + half, :, a:b].astype(F32)
        )

    other_rows = pl.ds(pl.multiple_of((row + 1 - 2 * h) * TB, TB), TB)

    def zxcopy(p, rows):
        s = phases[p][1]
        ref = dall.at[rows, pl.ds(s["off"], 2 * s["w"])]
        return rcopy(ref, ref, zx_s.at[p], zx_r.at[p], ydev)

    def ag_slice(s, half, zz):
        cols = pl.ds(s["off"] + half * s["w"], s["w"])
        if s["kind"] == "y":
            return dall.at[pl.ds(pl.multiple_of(zz * 2 * TB + h * TB, TB), TB), cols]
        return dall.at[pl.ds(pl.multiple_of(zz * 2 * TB, 2 * TB), 2 * TB), cols]

    def agcopy(p, k, d, t, arriving=False):
        s = phases[p][k]
        half = t % 2 if d == 0 else 1 - t % 2
        hops = t // 2 + (1 if arriving else 0)
        zz = lax.rem(z + (NZ - hops if d == 0 else hops), NZ)
        ref = ag_slice(s, half, zz)
        ss, rs = ((ay_s, ay_r), (az_s, az_r))[k]
        return rcopy(ref, ref, ss.at[p, d, t], rs.at[p, d, t], zdev[d])

    def yfcopy(p, d, t, arriving=False):
        s = phases[p][0]
        if d == 2:
            half, zz, n = t, z, t
        else:
            half = t % 2 if d == 0 else 1 - t % 2
            hops = t // 2 + 1
            zz = lax.rem(z + (NZ - hops if d == 0 else hops), NZ)
            n = 2 + d * 7 + t
        hh = 1 - h if arriving else h
        ref = dall.at[
            pl.ds(pl.multiple_of(zz * 2 * TB + hh * TB, TB), TB), pl.ds(s["off"] + half * s["w"], s["w"])
        ]
        return rcopy(ref, ref, yf_s.at[p, n], yf_r.at[p, n], ydev)

    def weight_grads(p, k):
        s = phases[p][k]

        @pl.loop(0, 2 * s["w"] // 256)
        def _(n):
            cols = pl.ds(pl.multiple_of(s["off"] + n * 256, 256), 256)
            gout[:, cols] = jnp.dot(xt[...], dall[:, cols], preferred_element_type=F32).astype(BF16)


    def start_own(p, k):
        for t in range(2):
            for d in range(2):
                agcopy(p, k, d, t).start()
        if k == 0:
            for half in range(2):
                yfcopy(p, 2, half).start()

    def take(p, k, d, t):
        agcopy(p, k, d, t, arriving=True).wait_recv()
        if t < 5:
            agcopy(p, k, d, t + 2).start()
        if k == 0:
            yfcopy(p, d, t).start()

    def y_done(p):
        for half in range(2):
            yfcopy(p, 2, half, arriving=True).wait_recv()
        for t in range(7):
            for d in range(2):
                yfcopy(p, d, t, arriving=True).wait_recv()

    for half in range(2):
        zfcopy(half).wait_recv()
    store_grads(0, ZW, z_pre)
    for p, (_, s) in enumerate(phases):
        if s["gcol"] + s["w"] <= ZW:
            zxcopy(p, my_rows).start()

    for d in range(2):
        for t in (5, 6):
            zycopy(d, t).wait_recv()
    for half in range(2):
        yecopy(0, half).wait_recv()
    store_grads(ZW, FL, y_pre)
    start_own(0, 0)
    for p, (_, s) in enumerate(phases):
        if s["gcol"] + s["w"] > ZW:
            zxcopy(p, my_rows).start()

    for p in range(len(phases)):
        if p == 0:
            zxcopy(0, other_rows).wait_recv()
            start_own(0, 1)
        for t in range(5):
            for k in range(2):
                for d in range(2):
                    take(p, k, d, t)
            if p and t == 1:
                weight_grads(p - 1, 1)
            if p and t == 3:
                y_done(p - 1)
                weight_grads(p - 1, 0)
        if p + 1 < len(phases):
            start_own(p + 1, 0)
            zxcopy(p + 1, other_rows).wait_recv()
            start_own(p + 1, 1)
        for t in (5, 6):
            for k in range(2):
                for d in range(2):
                    take(p, k, d, t)
    last = len(phases) - 1
    weight_grads(last, 1)
    y_done(last)

    own_copy(0, ldev).wait_send()
    for i in (2, 1, 3):
        own_copy(i, xdev(i)).wait_send()
        pass_copy(3 + i, xdev(i)).wait_send()
    for i in range(NZ):
        fcopy(jnp.int32(i)).wait_send()

    @pl.loop(0, 7)
    def _(t):
        for d in range(2):
            zzcopy(d, t).wait_send()
            zycopy(d, t).wait_send()

    @pl.loop(0, NZ)
    def _(rel):
        for half in range(2):
            yecopy(rel, half).wait_send()

    for half in range(2):
        zfcopy(half).wait_send()
    for p in range(len(phases)):
        zxcopy(p, my_rows).wait_send()
        for t in range(7):
            for d in range(2):
                for k in range(2):
                    agcopy(p, k, d, t).wait_send()
                yfcopy(p, d, t).wait_send()
        for half in range(2):
            yfcopy(p, 2, half).wait_send()


def finish(gout, xt, dall, gg_ref, gu_ref, late, osem):
    phases = streams()
    last = len(phases) - 1
    base = phases[last][0]["off"]
    copies = []

    def send(p, k, src, off):
        s = phases[p][k]
        w, g = s["w"], s["gcol"]
        for a, ref in enumerate((gg_ref, gu_ref)):
            c = pltpu.make_async_copy(src.at[:, pl.ds(off + a * w, w)], ref.at[:, pl.ds(g, w)], osem.at[p, k, a])
            c.start()
            copies.append(c)

    for p in range(last + 1):
        for k in range(2 if p < last else 1):
            send(p, 1 - k, gout, phases[p][1 - k]["off"])
    s = phases[last][0]

    @pl.loop(0, 2 * s["w"] // 256)
    def _(n):
        src = pl.ds(pl.multiple_of(base + n * 256, 256), 256)
        dst = pl.ds(pl.multiple_of(n * 256, 256), 256)
        late[:, dst] = jnp.dot(xt[...], dall[:, src], preferred_element_type=F32).astype(BF16)

    send(last, 0, late, 0)
    for c in copies:
        c.wait()


def local(tokens, gate_weight, up_weight, upstream):
    n = len(PHASES)
    dma = pltpu.SemaphoreType.DMA
    any_spec = pl.BlockSpec(memory_space=pl.ANY)
    vmem_spec = pl.BlockSpec(memory_space=pltpu.VMEM)
    gout, xt, dall = pl.pallas_call(
        kernel,
        out_shape=(pltpu.VMEM((DL, 2 * FL), BF16), pltpu.VMEM((DL, NT), BF16), pltpu.VMEM((NT, 2 * FL), BF16)),
        in_specs=[any_spec] * 4,
        out_specs=(vmem_spec,) * 3,
        scratch_shapes=[
            pltpu.VMEM((NT, DL), BF16),
            pltpu.VMEM((DL, 2 * FL), BF16),
            pltpu.VMEM((TB, FL), BF16),
            pltpu.VMEM((2, 7, 2 * TB, ZW), BF16),
            pltpu.VMEM((2, 9, 2 * TB, ZW), BF16),
            pltpu.VMEM((2, 7, TB, YW), BF16),
            pltpu.VMEM((2, 9, TB, YW), BF16),
            pltpu.VMEM((NZ, 2, TB, YW), F32),
            pltpu.VMEM((NZ, 2, TB, YW), BF16),
            pltpu.VMEM((NZ, 2, TB, YW), BF16),
            pltpu.VMEM((2, TB, ZW), F32),
            pltpu.VMEM((2, TB, ZW), BF16),
            pltpu.VMEM((2, TB, ZW), BF16),
            dma((5,)),
            dma((NZ,)), dma((NZ,)),
            dma((NZ,)), dma((NZ,)),
            dma((2, 7)), dma((2, 7)),
            dma((2, 7)), dma((2, 7)),
            dma((NZ, 2)), dma((NZ, 2)),
            dma((2,)), dma((2,)),
            dma((n, 2, 7)), dma((n, 2, 7)),
            dma((n, 2, 7)), dma((n, 2, 7)),
            dma((n, 16)), dma((n, 16)),
            dma((n,)), dma((n,)),
        ],
        compiler_params=pltpu.CompilerParams(
            collective_id=0, has_side_effects=True, vmem_limit_bytes=44 * 1024 * 1024
        ),
    )(tokens, gate_weight, up_weight, upstream)
    width = 2 * streams()[-1][0]["w"]
    return pl.pallas_call(
        finish,
        out_shape=(jax.ShapeDtypeStruct((DL, FL), BF16), jax.ShapeDtypeStruct((DL, FL), BF16)),
        in_specs=[vmem_spec] * 3,
        out_specs=(any_spec, any_spec),
        scratch_shapes=[pltpu.VMEM((DL, width), BF16), dma((n, 2, 2))],
        compiler_params=pltpu.CompilerParams(vmem_limit_bytes=4 * 1024 * 1024),
    )(gout, xt, dall)


def solution(mesh):
    return jax.shard_map(
        local,
        mesh=mesh,
        in_specs=(P("col", "row"), P("row", "col"), P("row", "col"), P("row", "col")),
        out_specs=(P("row", "col"), P("row", "col")),
        check_vma=False,
    )
```

```python
import functools

import jax
import jax.numpy as jnp
from jax import lax
from jax.experimental import pallas as pl
from jax.experimental.pallas import tpu as pltpu
from jax.sharding import PartitionSpec as P

MESH = pl.DeviceIdType.MESH
F32 = jnp.float32
BF16 = jnp.bfloat16

NZ = 8
TB = 64
NT = 1024
DL = 896
FL = 1664
LANE = 128

ZT, YT = 5, 8
ZW, YW = ZT * LANE, YT * LANE
PHASES = ((5, 3), (2, 3))
SPREAD = (((1, 0, 1),), ((1, 1, 3),), ((0, 0, 2),), ((0, 2, 4),), ((0, 4, 5),))


def streams():
    out = []
    off, zt, yt = 0, 0, sum(nz for _, nz in PHASES)
    for ny, nz in PHASES:
        y = dict(kind="y", off=off, w=ny * LANE, gcol=yt * LANE)
        off += 2 * ny * LANE
        yt += ny
        zs = dict(kind="z", off=off, w=nz * LANE, gcol=zt * LANE)
        off += 2 * nz * LANE
        zt += nz
        out.append((y, zs))
    return out


def rcopy(src, dst, ssem, rsem, dev):
    return pltpu.make_async_remote_copy(
        src_ref=src, dst_ref=dst, send_sem=ssem, recv_sem=rsem, device_id=dev, device_id_type=MESH
    )


def kernel(
    x_ref, wg_ref, wu_ref, up_ref, gout, xt, dall,
    xb, wb, ub, zsz, zrz, zsy, zry, yown, ysend, yrecv, zfin, zfs, zfr,
    wsem, g_s, g_r, f_s, f_r, zz_s, zz_r, zy_s, zy_r, ye_s, ye_r, zf_s, zf_r,
    ay_s, ay_r, az_s, az_r, yf_s, yf_r, zx_s, zx_r,
):
    row = lax.axis_index("row")
    col = lax.axis_index("col")
    z, h = lax.div(row, 2), lax.rem(row, 2)
    q, core = lax.div(col, 2), lax.rem(col, 2)
    zdev = ((lax.rem(z + 1, NZ) * 2 + h, col), (lax.rem(z + NZ - 1, NZ) * 2 + h, col))
    ydev = (z * 2 + 1 - h, col)
    cdev = (row, q * 2 + 1 - core)

    xx, yl = lax.div(q, 2), lax.rem(q, 2)
    ql = q + 1 - 2 * yl
    ldev = (row, ql * 2 + core)

    def xdev(i):
        return (row, (lax.rem(xx + i, 4) * 2 + yl) * 2 + core)

    loads = [
        pltpu.make_async_copy(wg_ref.at[:, pl.ds(ZW, YW)], wb.at[:, pl.ds(2 * ZW, YW)], wsem.at[2]),
        pltpu.make_async_copy(wu_ref.at[:, pl.ds(ZW, YW)], wb.at[:, pl.ds(2 * ZW + YW, YW)], wsem.at[3]),
        pltpu.make_async_copy(wg_ref.at[:, pl.ds(0, ZW)], wb.at[:, pl.ds(0, ZW)], wsem.at[0]),
        pltpu.make_async_copy(wu_ref.at[:, pl.ds(0, ZW)], wb.at[:, pl.ds(ZW, ZW)], wsem.at[1]),
        pltpu.make_async_copy(up_ref, ub, wsem.at[4]),
    ]

    def xrows(c):
        return xb.at[pl.ds(pl.multiple_of(c * TB, TB), TB), :]

    own_x = pltpu.make_async_copy(x_ref, xrows(col), g_r.at[q])
    own_x.start()
    for c in loads:
        c.start()

    barrier = pltpu.get_barrier_semaphore()
    partners = [zdev[0], zdev[1], ydev, cdev, ldev, xdev(1), xdev(2), xdev(3)]
    for dev in partners:
        pl.semaphore_signal(barrier, inc=1, device_id=dev, device_id_type=MESH)
    zrz[:, 0:2] = jnp.zeros((2, 2, 2 * TB, ZW), BF16)
    zry[:, 0:2] = jnp.zeros((2, 2, TB, YW), BF16)
    pl.semaphore_wait(barrier, len(partners))

    def own_copy(n, dev):
        return rcopy(x_ref, xrows(col), g_s.at[n], g_r.at[q], dev)

    def pass_copy(n, dev):
        rows = xrows(ql * 2 + core)
        return rcopy(rows, rows, g_s.at[n], g_r.at[ql], dev)

    def fcopy(b):
        rows = xrows(b * 2 + core)
        return rcopy(rows, rows, f_s.at[b], f_r.at[b], cdev)

    own_core = rcopy(x_ref, xrows(col), f_s.at[q], f_r.at[q], cdev)

    def fwait(b):
        rows = xrows(b * 2 + 1 - core)
        rcopy(rows, rows, f_s.at[b], f_r.at[b], cdev).wait_recv()

    def gwait(b):
        pltpu.make_async_copy(x_ref, xrows(b * 2 + core), g_r.at[b]).wait()

    def send_own():
        for i in (2, 1, 3):
            own_copy(i, xdev(i)).start()

    def send_neighbour():
        gwait(ql)
        for i in (2, 1, 3):
            pass_copy(3 + i, xdev(i)).start()
        fcopy(ql).start()

    own_copy(0, ldev).start()
    own_core.start()
    first = lax.rem(z + 4, NZ)

    @pl.when(ql == first)
    def _():
        send_neighbour()

    send_own()
    gwait(q)
    for c in loads:
        c.wait()
    fwait(q)

    def arrive(b):
        @pl.when(jnp.logical_and(b != q, b != ql))
        def _():
            gwait(b)
            fcopy(b).start()

    def arrived(b):
        @pl.when(jnp.logical_and(b != q, b != ql))
        def _():
            fwait(b)

    def tokens_for(zz):
        a = pl.multiple_of(zz * 2 * TB + (1 - h) * TB, TB)
        b = pl.multiple_of(zz * 2 * TB + h * TB, TB)
        return jnp.concatenate([xb[pl.ds(a, TB), :], xb[pl.ds(b, TB), :]], axis=0)

    def zzcopy(d, t):
        return rcopy(zsz.at[d, t], zrz.at[d, t + 2], zz_s.at[d, t], zz_r.at[d, t], zdev[d])

    def zycopy(d, t):
        return rcopy(zsy.at[d, t], zry.at[d, t + 2], zy_s.at[d, t], zy_r.at[d, t], zdev[d])

    def yecopy(rel, half):
        return rcopy(ysend.at[rel, half], yrecv.at[rel, half], ye_s.at[rel, half], ye_r.at[rel, half], ydev)

    def zfcopy(half):
        return rcopy(zfs.at[half], zfr.at[half], zf_s.at[half], zf_r.at[half], ydev)

    def half_of(d, t):
        return lax.rem(t, 2) if d == 0 else 1 - lax.rem(t, 2)

    def rel_of(d, t):
        o = 4 - lax.rem(t, 2) - lax.div(t, 2)
        return o if d == 0 else NZ - o

    def z_step(t):
        for d in range(2):
            half = half_of(d, t)
            xd = tokens_for(lax.rem(z + rel_of(d, t), NZ))
            cols = pl.ds(pl.multiple_of(half * ZW, LANE), ZW)
            acc = jnp.dot(xd, wb[:, cols], preferred_element_type=F32)

            @pl.when(t >= 2)
            def _():
                zzcopy(d, t - 2).wait_recv()

            zsz[d, t] = (acc + zrz[d, t].astype(F32)).astype(BF16)
            zzcopy(d, t).start()

    def y_part(rel):
        zz = lax.rem(z + rel, NZ)
        xd = tokens_for(zz)
        for half in range(2):
            acc = jnp.dot(xd, wb[:, 2 * ZW + half * YW : 2 * ZW + (half + 1) * YW], preferred_element_type=F32)
            ysend[rel, half] = acc[:TB].astype(BF16)
            yecopy(rel, half).start()
            yown[rel, half] = acc[TB:]
        rows = pl.ds(pl.multiple_of(zz * 2 * TB, 2 * TB), 2 * TB)
        xt[:, rows] = xb[rows, :].T

    def rel_at(j):
        odd = lax.rem(j, 2)
        return (1 - odd) * (4 + lax.div(j, 2)) + odd * lax.div(7 - j, 2)

    def y_step(j):
        rel = rel_at(j)

        @pl.when(jnp.logical_and(rel != rel_q, rel != rel_ql))
        def _():
            y_part(rel)

    def block(j):
        return lax.rem(z + rel_at(jnp.int32(j)), NZ)

    rel_q = lax.rem(q + NZ - z, NZ)
    rel_ql = lax.rem(ql + NZ - z, NZ)
    y_part(rel_q)

    @pl.when(ql != first)
    def _():
        send_neighbour()

    fwait(ql)
    y_part(rel_ql)

    arrive(block(0))
    arrived(block(0))
    z_step(jnp.int32(0))
    for j in range(1, NZ):
        arrive(block(j))
    y_step(jnp.int32(0))
    for j in range(1, NZ):
        arrived(block(j))

    @pl.loop(1, NZ - 1)
    def _(t):
        z_step(t)
        y_step(t)

    y_step(jnp.int32(NZ - 1))

    def yz_step(t):
        for d in range(2):
            half = half_of(d, t)
            rel = rel_of(d, t)
            yecopy(rel, half).wait_recv()

            @pl.when(t >= 2)
            def _():
                zycopy(d, t - 2).wait_recv()

            acc = yown[rel, half] + yrecv[rel, half].astype(F32) + zry[d, t].astype(F32)
            zsy[d, t] = acc.astype(BF16)
            zycopy(d, t).start()

    @pl.loop(0, 3)
    def _(t):
        yz_step(t)

    for d in range(2):
        for t in (5, 6):
            zzcopy(d, t).wait_recv()
    xd = tokens_for(z)
    for half in range(2):
        acc = jnp.dot(xd, wb[:, half * ZW : (half + 1) * ZW], preferred_element_type=F32)
        acc = acc + zrz[0, 8 - half].astype(F32) + zrz[1, 7 + half].astype(F32)
        zfs[half] = acc[:TB].astype(BF16)
        zfcopy(half).start()
        zfin[half] = acc[TB:]

    @pl.loop(3, NZ - 1)
    def _(t):
        yz_step(t)

    my_rows = pl.ds(pl.multiple_of(row * TB, TB), TB)
    phases = streams()

    def store_grads(lo, hi, pre):
        for s in (s for phase in phases for s in phase):
            a, b = max(lo, s["gcol"]), min(hi, s["gcol"] + s["w"])
            if a >= b:
                continue
            gate, up = pre(0, a - lo, b - lo), pre(1, a - lo, b - lo)
            off = s["off"] + a - s["gcol"]
            u = ub[:, a:b].astype(F32)
            squash = jax.nn.sigmoid(gate)
            dall[my_rows, off : off + b - a] = (
                u * up * squash * (1.0 + gate * (1.0 - squash))
            ).astype(BF16)
            off += s["w"]
            dall[my_rows, off : off + b - a] = (u * gate * squash).astype(BF16)

    def z_pre(half, a, b):
        return zfin[half, :, a:b] + zfr[half, :, a:b].astype(F32)

    def y_pre(half, a, b):
        return (
            yown[0, half, :, a:b] + yrecv[0, half, :, a:b].astype(F32)
            + zry[0, 8 - half, :, a:b].astype(F32) + zry[1, 7 + half, :, a:b].astype(F32)
        )

    other_rows = pl.ds(pl.multiple_of((row + 1 - 2 * h) * TB, TB), TB)

    def zxcopy(p, rows):
        s = phases[p][1]
        ref = dall.at[rows, pl.ds(s["off"], 2 * s["w"])]
        return rcopy(ref, ref, zx_s.at[p], zx_r.at[p], ydev)

    def ag_slice(s, half, zz):
        cols = pl.ds(s["off"] + half * s["w"], s["w"])
        if s["kind"] == "y":
            return dall.at[pl.ds(pl.multiple_of(zz * 2 * TB + h * TB, TB), TB), cols]
        return dall.at[pl.ds(pl.multiple_of(zz * 2 * TB, 2 * TB), 2 * TB), cols]

    def agcopy(p, k, d, t, arriving=False):
        s = phases[p][k]
        half = t % 2 if d == 0 else 1 - t % 2
        hops = t // 2 + (1 if arriving else 0)
        zz = lax.rem(z + (NZ - hops if d == 0 else hops), NZ)
        ref = ag_slice(s, half, zz)
        ss, rs = ((ay_s, ay_r), (az_s, az_r))[k]
        return rcopy(ref, ref, ss.at[p, d, t], rs.at[p, d, t], zdev[d])

    def yfcopy(p, d, t, arriving=False):
        s = phases[p][0]
        if d == 2:
            half, zz, n = t, z, t
        else:
            half = t % 2 if d == 0 else 1 - t % 2
            hops = t // 2 + 1
            zz = lax.rem(z + (NZ - hops if d == 0 else hops), NZ)
            n = 2 + d * 7 + t
        hh = 1 - h if arriving else h
        ref = dall.at[
            pl.ds(pl.multiple_of(zz * 2 * TB + hh * TB, TB), TB), pl.ds(s["off"] + half * s["w"], s["w"])
        ]
        return rcopy(ref, ref, yf_s.at[p, n], yf_r.at[p, n], ydev)

    def weight_grads(p, k, lo=0, hi=None):
        s = phases[p][k]

        @pl.loop(lo, 2 * s["w"] // 256 if hi is None else hi)
        def _(n):
            cols = pl.ds(pl.multiple_of(s["off"] + n * 256, 256), 256)
            gout[:, cols] = jnp.dot(xt[...], dall[:, cols], preferred_element_type=F32).astype(BF16)


    def start_own(p, k):
        for t in range(2):
            for d in range(2):
                agcopy(p, k, d, t).start()
        if k == 0:
            for half in range(2):
                yfcopy(p, 2, half).start()

    def take(p, k, d, t):
        agcopy(p, k, d, t, arriving=True).wait_recv()
        if t < 5:
            agcopy(p, k, d, t + 2).start()
        if k == 0:
            yfcopy(p, d, t).start()

    def y_done(p):
        for half in range(2):
            yfcopy(p, 2, half, arriving=True).wait_recv()
        for t in range(7):
            for d in range(2):
                yfcopy(p, d, t, arriving=True).wait_recv()

    for half in range(2):
        zfcopy(half).wait_recv()
    store_grads(0, ZW, z_pre)
    for p, (_, s) in enumerate(phases):
        if s["gcol"] + s["w"] <= ZW:
            zxcopy(p, my_rows).start()

    for d in range(2):
        for t in (5, 6):
            zycopy(d, t).wait_recv()
    for half in range(2):
        yecopy(0, half).wait_recv()
    store_grads(ZW, FL, y_pre)
    start_own(0, 0)
    for p, (_, s) in enumerate(phases):
        if s["gcol"] + s["w"] > ZW:
            zxcopy(p, my_rows).start()

    for p in range(len(phases)):
        if p == 0:
            zxcopy(0, other_rows).wait_recv()
            start_own(0, 1)
        for t in range(5):
            for k in range(2):
                for d in range(2):
                    take(p, k, d, t)
            if p:
                for k, lo, hi in SPREAD[t]:
                    if k == 0 and lo == 0:
                        y_done(p - 1)
                    weight_grads(p - 1, k, lo, hi)
        if p + 1 < len(phases):
            start_own(p + 1, 0)
            zxcopy(p + 1, other_rows).wait_recv()
            start_own(p + 1, 1)
        for t in (5, 6):
            for k in range(2):
                for d in range(2):
                    take(p, k, d, t)
    last = len(phases) - 1
    weight_grads(last, 1)
    y_done(last)

    own_copy(0, ldev).wait_send()
    for i in (2, 1, 3):
        own_copy(i, xdev(i)).wait_send()
        pass_copy(3 + i, xdev(i)).wait_send()
    for i in range(NZ):
        fcopy(jnp.int32(i)).wait_send()

    @pl.loop(0, 7)
    def _(t):
        for d in range(2):
            zzcopy(d, t).wait_send()
            zycopy(d, t).wait_send()

    @pl.loop(0, NZ)
    def _(rel):
        for half in range(2):
            yecopy(rel, half).wait_send()

    for half in range(2):
        zfcopy(half).wait_send()
    for p in range(len(phases)):
        zxcopy(p, my_rows).wait_send()
        for t in range(7):
            for d in range(2):
                for k in range(2):
                    agcopy(p, k, d, t).wait_send()
                yfcopy(p, d, t).wait_send()
        for half in range(2):
            yfcopy(p, 2, half).wait_send()


def finish(gout, xt, dall, gg_ref, gu_ref, late, osem):
    phases = streams()
    last = len(phases) - 1
    base = phases[last][0]["off"]
    copies = []

    def send(p, k, src, off):
        s = phases[p][k]
        w, g = s["w"], s["gcol"]
        for a, ref in enumerate((gg_ref, gu_ref)):
            c = pltpu.make_async_copy(src.at[:, pl.ds(off + a * w, w)], ref.at[:, pl.ds(g, w)], osem.at[p, k, a])
            c.start()
            copies.append(c)

    for p in range(last + 1):
        for k in range(2 if p < last else 1):
            send(p, 1 - k, gout, phases[p][1 - k]["off"])
    s = phases[last][0]

    @pl.loop(0, 2 * s["w"] // 256)
    def _(n):
        src = pl.ds(pl.multiple_of(base + n * 256, 256), 256)
        dst = pl.ds(pl.multiple_of(n * 256, 256), 256)
        late[:, dst] = jnp.dot(xt[...], dall[:, src], preferred_element_type=F32).astype(BF16)

    send(last, 0, late, 0)
    for c in copies:
        c.wait()


def local(tokens, gate_weight, up_weight, upstream):
    n = len(PHASES)
    dma = pltpu.SemaphoreType.DMA
    any_spec = pl.BlockSpec(memory_space=pl.ANY)
    vmem_spec = pl.BlockSpec(memory_space=pltpu.VMEM)
    gout, xt, dall = pl.pallas_call(
        kernel,
        out_shape=(pltpu.VMEM((DL, 2 * FL), BF16), pltpu.VMEM((DL, NT), BF16), pltpu.VMEM((NT, 2 * FL), BF16)),
        in_specs=[any_spec] * 4,
        out_specs=(vmem_spec,) * 3,
        scratch_shapes=[
            pltpu.VMEM((NT, DL), BF16),
            pltpu.VMEM((DL, 2 * FL), BF16),
            pltpu.VMEM((TB, FL), BF16),
            pltpu.VMEM((2, 7, 2 * TB, ZW), BF16),
            pltpu.VMEM((2, 9, 2 * TB, ZW), BF16),
            pltpu.VMEM((2, 7, TB, YW), BF16),
            pltpu.VMEM((2, 9, TB, YW), BF16),
            pltpu.VMEM((NZ, 2, TB, YW), F32),
            pltpu.VMEM((NZ, 2, TB, YW), BF16),
            pltpu.VMEM((NZ, 2, TB, YW), BF16),
            pltpu.VMEM((2, TB, ZW), F32),
            pltpu.VMEM((2, TB, ZW), BF16),
            pltpu.VMEM((2, TB, ZW), BF16),
            dma((5,)),
            dma((NZ,)), dma((NZ,)),
            dma((NZ,)), dma((NZ,)),
            dma((2, 7)), dma((2, 7)),
            dma((2, 7)), dma((2, 7)),
            dma((NZ, 2)), dma((NZ, 2)),
            dma((2,)), dma((2,)),
            dma((n, 2, 7)), dma((n, 2, 7)),
            dma((n, 2, 7)), dma((n, 2, 7)),
            dma((n, 16)), dma((n, 16)),
            dma((n,)), dma((n,)),
        ],
        compiler_params=pltpu.CompilerParams(
            collective_id=0, has_side_effects=True, vmem_limit_bytes=44 * 1024 * 1024
        ),
    )(tokens, gate_weight, up_weight, upstream)
    width = 2 * streams()[-1][0]["w"]
    return pl.pallas_call(
        finish,
        out_shape=(jax.ShapeDtypeStruct((DL, FL), BF16), jax.ShapeDtypeStruct((DL, FL), BF16)),
        in_specs=[vmem_spec] * 3,
        out_specs=(any_spec, any_spec),
        scratch_shapes=[pltpu.VMEM((DL, width), BF16), dma((n, 2, 2))],
        compiler_params=pltpu.CompilerParams(vmem_limit_bytes=4 * 1024 * 1024),
    )(gout, xt, dall)


def solution(mesh):
    return jax.shard_map(
        local,
        mesh=mesh,
        in_specs=(P("col", "row"), P("row", "col"), P("row", "col"), P("row", "col")),
        out_specs=(P("row", "col"), P("row", "col")),
        check_vma=False,
    )
```
